256 devices in a mesh: grp: 8 (over x, core), tok: 32 (over y, z).
Axes of the slice: x: 4, y: 4, z: 8, core: 2. Of those that a mesh axis runs over, the one named last changes fastest.
Arguments:
- hidden_in: bfloat16 [12288, 2048], P('tok', 'grp'), may hold values from -6 to 6
- w_qkv: float32 [2048, 6144], P(('grp', 'tok')), may hold values from -1 to 1
- w_out: float32 [2048, 2048], P(('grp', 'tok')), may hold values from -0.125 to 0.125
- qkv_bias: float32 [6144], P('grp'), may hold values from -3 to 3
- out_bias: float32 [2048], P('grp'), may hold values from -3 to 3
- ln_gain: float32 [2048], replicated, may hold values from 0.5 to 1.5
- ln_bias: float32 [2048], replicated, may hold values from -2 to 2
- cache_k: bfloat16 [8192, 2048], P('tok', 'grp'), may hold values from -300 to 300
- cache_v: bfloat16 [8192, 2048], P('tok', 'grp'), may hold values from -6 to 6
- prompt_lengths: int32 [8], replicated, may hold values from 1 to 9216, 12288 in all
- cache_lengths: int32 [8], replicated, may hold values from 0 to 256, as said below
- cache_holders: int32 [8], replicated, may hold values from 0 to 31, as said below
Outputs:
- layer_out: bfloat16 [12288, 2048], P('tok', 'grp')
The draws below stay inside these ranges and needn't reach their ends.
Inputs may be any that keep to these rules, and one draw needn't show every extreme that they name: `prompt_lengths`: the lengths sum to 12288 and the longest is exactly 9216. `cache_lengths`: 4 prompts have a cache of 1 to 256 positions and the others none; some prompt has exactly 256. `cache_holders`: the 8 holders are distinct.
All inputs are finite; a program needn't handle non-finite values.
Results may differ from the reference program's by a relative error of at most 0.013.
Values may be sent and summed in bfloat16 or wider, within the bound.
No kernel may reach another device: no remote copies, remote signals or barrier semaphores. Data moves between devices by JAX's collectives and lax.ppermute only.
A program may use at most 128 MiB of HBM per device.

```python
import math
import jax
import jax.numpy as jnp
import numpy as np
from jax import lax

D = 2048
H = 8
HD = 256
ROT = 64
P_SIZE = 8
CACHE_DEV = 256
TOKENS = 12288
MAXLEN = 9216
CACHE_SLOTS = 8192


def draw_w_qkv(key, part):
    column = jnp.arange(3 * D, dtype=jnp.int32)
    part_id = column // HD % 3
    spread = jnp.where(part_id < 2, 1.8, 1.0).astype(jnp.float32) * float(D) ** (-0.5)
    base = jnp.clip(jax.random.normal(jax.random.fold_in(key, 42), (D, 3 * D), jnp.float32), -6.0, 6.0)
    return base * spread[None, :]


def draw_cache_k(key, part):
    return (1.9 * jnp.clip(jax.random.normal(jax.random.fold_in(key, 13), (CACHE_SLOTS, D), jnp.float32), -6.0, 6.0)).astype(jnp.bfloat16)


def draw_cache_lengths(key, part):
    order = jax.random.permutation(jax.random.fold_in(key, 21), P_SIZE)
    lengths = jax.random.randint(jax.random.fold_in(key, 22), (P_SIZE,), 1, CACHE_DEV + 1)
    lengths = jnp.where(order == 0, CACHE_DEV, lengths)
    return jnp.where(order < P_SIZE // 2, lengths, 0).astype(jnp.int32)


def draw_cache_holders(key, part):
    devices = CACHE_SLOTS // CACHE_DEV
    inner = 1 + jax.random.permutation(jax.random.fold_in(key, 31), devices - 2)[:P_SIZE - 2]
    picks = jnp.concatenate([jnp.array([0, devices - 1], jnp.int32), inner.astype(jnp.int32)])
    return picks[jax.random.permutation(jax.random.fold_in(key, 32), P_SIZE)].astype(jnp.int32)


def block_scale(own_key, shape, cuts, low, largest):
    level = 1.0
    for dim, shards_of in cuts:
        steps = jax.random.uniform(jax.random.fold_in(jax.random.fold_in(own_key, 6), dim), (shards_of,), jnp.float32, low / len(cuts), largest / len(cuts))
        level = level * jnp.repeat(jnp.exp(steps), shape[dim] // shards_of).reshape((-1,) + (1,) * (len(shape) - 1 - dim))
    return level


def length_profile(count, total, reach, slope):
    portions = [(1 << 20) // math.isqrt(grade ** slope) + 1 for grade in range(2, count + 1)]
    spare, counts = total - reach - (count - 1), [1] * (count - 1)
    while spare > 0:
        candidates = [i for i in range(count - 1) if counts[i] < reach]
        pool, remaining = sum([portions[i] for i in candidates]), spare
        for i in candidates:
            addition = min(reach - counts[i], max(1, remaining * portions[i] // pool), spare)
            counts[i] = counts[i] + addition
            spare = spare - addition
    return np.array([reach] + counts)


def uneven_parts(stream_key, number_of, total, limit, lean):
    if number_of == 2:
        one = jax.random.randint(stream_key, (), max(1, total - limit), min(limit, total - 1) + 1)
        return jnp.stack([one, total - one])
    sizes = jnp.asarray(length_profile(number_of, total, limit, lean), jnp.int32)
    couples = (number_of - 1) // 2
    source_of, receiver = sizes[1:1 + 2 * couples:2], sizes[2:2 + 2 * couples:2]
    slack = jnp.minimum(source_of - 1, limit - receiver)
    passed = jax.random.randint(jax.random.fold_in(stream_key, 1), (couples,), 0, 1 << 20) % (slack + 1)
    sizes = sizes.at[1:1 + 2 * couples:2].set(source_of - passed).at[2:2 + 2 * couples:2].set(receiver + passed)
    return sizes[jax.random.permutation(jax.random.fold_in(stream_key, 2), number_of)]


def scatter_about(own_key, dims, deviation, bound, cuts=(), kind=jnp.bfloat16):
    loudness = block_scale(own_key, dims, cuts, -0.22, 0.18) if cuts else 1.0
    values = jax.random.normal(own_key, dims, jnp.float32) * deviation * loudness
    return jnp.minimum(jnp.maximum(values, -bound), bound).astype(kind)


def setup_inputs(seed: int = 0) -> dict:
    seeds = jax.random.split(jax.random.key(seed), 13)
    return {
        "hidden_in": scatter_about(seeds[0], (TOKENS, D), 1.0, 6.0, ((0, 32), (1, 8))),
        "w_qkv": draw_w_qkv(jax.random.fold_in(seeds[12], 71), 0),
        "w_out": scatter_about(seeds[2], (D, D), D ** -0.5, 0.125, ((0, 256),), jnp.float32),
        "qkv_bias": scatter_about(seeds[3], (3 * D,), 0.5, 3.0, ((0, 8),), jnp.float32),
        "out_bias": scatter_about(seeds[4], (D,), 0.5, 3.0, ((0, 8),), jnp.float32),
        "ln_gain": jnp.clip(1.0 + 0.1 * jax.random.normal(seeds[5], (D,), jnp.float32), 0.5, 1.5),
        "ln_bias": scatter_about(seeds[6], (D,), 0.3, 2.0, (), jnp.float32),
        "cache_k": draw_cache_k(jax.random.fold_in(seeds[12], 71), 0),
        "cache_v": scatter_about(seeds[8], (CACHE_SLOTS, D), 1.0, 6.0, ((0, 32), (1, 8))),
        "prompt_lengths": uneven_parts(seeds[9], P_SIZE, TOKENS, MAXLEN, 2).astype(jnp.int32),
        "cache_lengths": draw_cache_lengths(jax.random.fold_in(seeds[12], 71), 0),
        "cache_holders": draw_cache_holders(jax.random.fold_in(seeds[12], 71), 0),
    }


def layer_norm(hidden, ln_gain, ln_bias):
    widened = hidden.astype(jnp.float32)
    row_mean = lax.optimization_barrier(jnp.mean(widened, axis=-1, keepdims=True))
    centred = widened - row_mean
    row_var = lax.optimization_barrier(jnp.mean(centred * centred, axis=-1, keepdims=True))
    return centred * lax.rsqrt(row_var + 1e-05) * ln_gain + ln_bias

def rotate(values_in, position):
    half_rot = ROT // 2
    frequency = 10000.0 ** (-2.0 * jnp.arange(half_rot, dtype=jnp.float32) / ROT)
    angles = position.astype(jnp.float32)[:, None] * frequency[None, :]
    cosine = jnp.cos(angles)[:, None, :]
    sine_part = jnp.sin(angles)[:, None, :]
    first_half = values_in[..., :half_rot]
    second_half = values_in[..., half_rot:ROT]
    return jnp.concatenate([first_half * cosine - second_half * sine_part, second_half * cosine + first_half * sine_part, values_in[..., ROT:]], axis=-1)

def token_info(tok_index, prompt_lengths, cache_lengths):
    prompt_ends = jnp.cumsum(prompt_lengths).astype(jnp.int32)
    prompt_starts = prompt_ends - prompt_lengths
    prompt = lax.optimization_barrier(jnp.sum((tok_index[:, None] >= prompt_ends[None, :]).astype(jnp.int32), axis=1)).astype(jnp.int32)
    onehot = prompt[:, None] == jnp.arange(P_SIZE, dtype=jnp.int32)[None, :]
    first_tok = lax.optimization_barrier(jnp.sum(jnp.where(onehot, prompt_starts[None, :], 0), axis=1)).astype(jnp.int32)
    offset = lax.optimization_barrier(jnp.sum(jnp.where(onehot, cache_lengths[None, :], 0), axis=1)).astype(jnp.int32)
    return (prompt, offset + tok_index - first_tok)

def slot_owner(slot_ids, slots_each, cache_lengths, cache_holders):
    slot_device = slot_ids // slots_each
    slot_local = slot_ids % slots_each
    matched = (slot_device[:, None] == cache_holders[None, :]) & (slot_local[:, None] < cache_lengths[None, :])
    labels = jnp.arange(P_SIZE, dtype=jnp.int32)[None, :] + 1
    return (lax.optimization_barrier(jnp.sum(jnp.where(matched, labels, 0), axis=1)) - 1).astype(jnp.int32)

def reference(hidden_in, w_qkv, w_out, qkv_bias, out_bias, ln_gain, ln_bias, cache_k, cache_v, prompt_lengths, cache_lengths, cache_holders):
    tok_index = jnp.arange(TOKENS, dtype=jnp.int32)
    prompt, position = token_info(tok_index, prompt_lengths, cache_lengths)
    normed = layer_norm(hidden_in, ln_gain, ln_bias).astype(jnp.bfloat16)
    server_qkv = w_qkv.astype(jnp.bfloat16)
    server_out = w_out.astype(jnp.bfloat16)
    joined = jnp.dot(normed, server_qkv, preferred_element_type=jnp.float32) + qkv_bias
    joined = joined.reshape(TOKENS, H, 3, HD)
    query = rotate(joined[:, :, 0], position).astype(jnp.bfloat16)
    key_new = rotate(joined[:, :, 1], position).astype(jnp.bfloat16)
    value_new = joined[:, :, 2].astype(jnp.bfloat16)
    owners = slot_owner(jnp.arange(CACHE_SLOTS, dtype=jnp.int32), CACHE_DEV, cache_lengths, cache_holders)

    def compact(table):

        def take(holder):
            return lax.dynamic_slice_in_dim(table, (holder * CACHE_DEV).astype(jnp.int32), CACHE_DEV, 0)
        return jax.vmap(take)(cache_holders)
    cache_keys = compact(cache_k).reshape(P_SIZE * CACHE_DEV, H, HD)
    cache_values = compact(cache_v).reshape(P_SIZE * CACHE_DEV, H, HD)
    cache_owner = compact(owners[:, None]).reshape(P_SIZE * CACHE_DEV)
    pad_keys = jnp.concatenate([jnp.zeros((MAXLEN, H, HD), jnp.bfloat16), key_new], axis=0)
    pad_values = jnp.concatenate([jnp.zeros((MAXLEN, H, HD), jnp.bfloat16), value_new], axis=0)
    pad_prompt = jnp.concatenate([jnp.full((MAXLEN,), -1, jnp.int32), prompt], axis=0)
    pad_index = jnp.concatenate([jnp.arange(MAXLEN, dtype=jnp.int32) - MAXLEN, tok_index], axis=0)
    block_rows = math.gcd(TOKENS, 512)
    scale = 1.0 / math.sqrt(HD)
    cache_index = jnp.full((P_SIZE * CACHE_DEV,), -1, jnp.int32)

    def one_block(block_id):
        first_row = (block_id * block_rows).astype(jnp.int32)
        q_block = lax.dynamic_slice_in_dim(query, first_row, block_rows, 0)
        q_prompt = lax.dynamic_slice_in_dim(prompt, first_row, block_rows, 0)
        q_index = lax.dynamic_slice_in_dim(tok_index, first_row, block_rows, 0)
        k_block = lax.dynamic_slice_in_dim(pad_keys, first_row, MAXLEN + block_rows, 0)
        v_block = lax.dynamic_slice_in_dim(pad_values, first_row, MAXLEN + block_rows, 0)
        p_block = lax.dynamic_slice_in_dim(pad_prompt, first_row, MAXLEN + block_rows, 0)
        i_block = lax.dynamic_slice_in_dim(pad_index, first_row, MAXLEN + block_rows, 0)
        keys_all = jnp.concatenate([cache_keys, k_block], axis=0).astype(jnp.float32)
        values_all = jnp.concatenate([cache_values, v_block], axis=0).astype(jnp.float32)
        key_prompt = jnp.concatenate([cache_owner, p_block], axis=0)
        key_index = jnp.concatenate([cache_index, i_block], axis=0)
        allowed = (key_prompt[None, :] == q_prompt[:, None]) & (key_index[None, :] <= q_index[:, None])
        allowed3 = allowed[:, None, :]
        scores = jnp.einsum('qhd,khd->qhk', q_block.astype(jnp.float32), keys_all) * scale
        row_max = lax.optimization_barrier(jnp.max(jnp.where(allowed3, scores, -1e+30), axis=-1, keepdims=True))
        weights_f = jnp.exp(jnp.where(allowed3, scores - row_max, -1e+30))
        totals = lax.optimization_barrier(jnp.sum(weights_f, axis=-1))
        weights = lax.optimization_barrier(weights_f.astype(jnp.bfloat16))
        mixed = jnp.einsum('qhk,khd->qhd', weights.astype(jnp.float32), values_all)
        return (mixed / totals[..., None]).astype(jnp.bfloat16).reshape(block_rows, D)
    attended = lax.map(one_block, jnp.arange(TOKENS // block_rows, dtype=jnp.int32)).reshape(TOKENS, D)
    projected = jnp.dot(attended, server_out, preferred_element_type=jnp.float32)
    return (hidden_in.astype(jnp.float32) + projected + out_bias).astype(jnp.bfloat16)
```

```python
import math

import jax
import jax.numpy as jnp
from jax import lax
from jax.experimental import pallas as pl
from jax.experimental.pallas import tpu as pltpu
from jax.sharding import Mesh, PartitionSpec as P

HD = 256
ROT = 64
P_SIZE = 8
NX, NC, NY, NZ = 4, 2, 4, 8
SIZES = {"x": NX, "c": NC, "y": NY, "z": NZ}
NEG = -1e30
SCALE2 = math.log2(math.e) / math.sqrt(HD)
BF = jnp.bfloat16
F32 = jnp.float32


def shift(value, axis, by):
    n = SIZES[axis]
    return lax.ppermute(value, axis, [(i, (i + by) % n) for i in range(n)])


def ring4(value, axis):
    half = value.shape[0] // 2
    right = shift(value, axis, 1)
    left = shift(value, axis, -1)
    far_a = shift(right[:half], axis, 1)
    far_b = shift(left[half:], axis, -1)
    return [value, right, left, far_a, far_b]


def ring8(values, axis):
    outs = [[v] for v in values]
    rights = list(values)
    lefts = list(values)
    for _ in range(3):
        rights = [shift(v, axis, 1) for v in rights]
        lefts = [shift(v, axis, -1) for v in lefts]
        for o, r, l in zip(outs, rights, lefts):
            o += [r, l]
    for o, r, l in zip(outs, rights, lefts):
        half = r.shape[0] // 2
        o += [shift(r[:half], axis, 1), shift(l[half:], axis, -1)]
    return outs


RING8 = (0, -1, 1, -2, 2, -3, 3, 4)
RING4 = (0, -1, 1, 2)


def vmem():
    return pl.BlockSpec(memory_space=pltpu.VMEM)


def smem():
    return pl.BlockSpec(memory_space=pltpu.SMEM)


def hbm():
    return pl.BlockSpec(memory_space=pl.ANY)


def params(mb=48):
    return pltpu.CompilerParams(vmem_limit_bytes=mb << 20)


def norm_kernel(pos, mine, other, gain, bias, out):
    rows = mine.shape[1]
    total = jnp.zeros((rows, 1), F32)
    for ref in (mine, other):
        for k in range(NX):
            total += jnp.sum(ref[k].astype(F32), axis=1, keepdims=True)
    mean = total * (1.0 / (NX * NC * HD))
    square = jnp.zeros((rows, 1), F32)
    for ref in (mine, other):
        for k in range(NX):
            d = ref[k].astype(F32) - mean
            square += jnp.sum(d * d, axis=1, keepdims=True)
    scale = lax.rsqrt(square * (1.0 / (NX * NC * HD)) + 1e-05)
    for flip, ref in ((0, mine), (1, other)):
        for k in range(NX):
            g = lax.rem(pos[0] + RING4[k] + NX, NX) * NC + (pos[1] ^ flip)
            d = ref[k].astype(F32) - mean
            out[g] = (d * scale * gain[g] + bias[g]).astype(BF)


def norm_call(pos, mine, other, gain, bias):
    rows = mine.shape[1]
    return pl.pallas_call(
        norm_kernel,
        out_shape=jax.ShapeDtypeStruct((NX * NC, rows, HD), BF),
        in_specs=[smem(), vmem(), vmem(), vmem(), vmem()],
        out_specs=vmem(),
        compiler_params=params(),
        name="norm",
    )(pos, mine, other, gain, bias)


def proj_kernel(pos, normed, bias, cosw, sinl, sinr, y0, y1, y2, y3a, y3b, q_out, k_out, v_out, wbuf, sem):
    def pieces():
        for k, ref in enumerate((y0, y1, y2, None)):
            row = lax.rem(pos[2] + RING4[k] + NY, NY)
            for p in range(NZ):
                t = row * NZ + lax.rem(pos[3] + RING8[p] + NZ, NZ)
                if ref is not None:
                    yield ref.at[p], t
                else:
                    far = y3a if p < NZ // 2 else y3b
                    yield far.at[p % (NZ // 2)], t

    copies = [pltpu.make_async_copy(src, wbuf.at[:, t], sem.at[i]) for i, (src, t) in enumerate(pieces())]
    for c in copies:
        c.start()
    for c in copies:
        c.wait()
    rows = normed.shape[1]
    joined = jnp.broadcast_to(bias[...], (rows, 3 * HD))
    for g in range(NX * NC):
        w = wbuf[g].reshape(NY * NZ * 8, 3 * HD)
        joined += jnp.dot(normed[g], w, preferred_element_type=F32)

    def rotated(part):
        head = part[:, :128]
        back = pltpu.roll(head, 128 - ROT // 2, 1)
        fwd = pltpu.roll(head, ROT // 2, 1)
        return head * cosw[...] + back * sinl[...] + fwd * sinr[...]

    q = joined[:, :HD]
    k = joined[:, HD : 2 * HD]
    q_out[:, :128] = rotated(q).astype(BF)
    q_out[:, 128:] = q[:, 128:].astype(BF)
    k_out[:, :128] = rotated(k).astype(BF)
    k_out[:, 128:] = k[:, 128:].astype(BF)
    v_out[...] = jnp.transpose(joined[:, 2 * HD :]).astype(BF)


def proj_call(pos, normed, bias, tables, blocks):
    rows = normed.shape[1]
    return pl.pallas_call(
        proj_kernel,
        out_shape=(
            jax.ShapeDtypeStruct((rows, HD), BF),
            jax.ShapeDtypeStruct((rows, HD), BF),
            jax.ShapeDtypeStruct((HD, rows), BF),
        ),
        in_specs=[smem()] + [vmem()] * 5 + [hbm()] * 5,
        out_specs=(vmem(), vmem(), vmem()),
        scratch_shapes=[
            pltpu.VMEM((NX * NC, NY * NZ, 8, 3 * HD), BF),
            pltpu.SemaphoreType.DMA((NY * NZ,)),
        ],
        compiler_params=params(),
        name="proj",
    )(pos, normed, bias, *tables, *blocks)


def attend_kernel(pos, plen, clen, hold, *refs):
    rows = 384
    nq, nk = 5, 9
    q_in = refs[:nq]
    k_in = refs[nq : nq + nk]
    v_in = refs[nq + nk : nq + 2 * nk]
    cache_in, out = refs[nq + 2 * nk : nq + 2 * nk + 2]
    qb, kb, vb, cb, stat, acc, qsem, ksem, vsem, csem = refs[nq + 2 * nk + 2 :]
    hr, hd = rows // 2, HD // 2

    qc = [pltpu.make_async_copy(q_in[i], qb.at[i], qsem.at[i]) for i in range(3)]
    qc += [pltpu.make_async_copy(q_in[3 + i], qb.at[3, pl.ds(i * hr, hr)], qsem.at[3 + i]) for i in range(2)]
    kc = [pltpu.make_async_copy(k_in[i], kb.at[i], ksem.at[i]) for i in range(7)]
    kc += [pltpu.make_async_copy(k_in[7 + i], kb.at[7, pl.ds(i * hr, hr)], ksem.at[7 + i]) for i in range(2)]
    vc = [pltpu.make_async_copy(v_in[i], vb.at[i], vsem.at[i]) for i in range(7)]
    vc += [pltpu.make_async_copy(v_in[7 + i], vb.at[7, pl.ds(i * hd, hd)], vsem.at[7 + i]) for i in range(2)]
    cc = pltpu.make_async_copy(cache_in, cb, csem)
    every = qc + kc + vc + [cc]
    for c in every:
        c.start()

    starts, ends = [], []
    run = jnp.int32(0)
    for p in range(P_SIZE):
        starts.append(run)
        run = run + plen[p]
        ends.append(run)
    for c in every:
        c.wait()
    lane = lax.broadcasted_iota(jnp.int32, (1, rows), 1)

    def fold(q, k, vt, allowed):
        s = lax.dot_general(k, q, (((1,), (1,)), ((), ())), preferred_element_type=F32)
        if allowed is not None:
            s = jnp.where(allowed, s, NEG)
        m_old = stat[0:1]
        m_new = jnp.maximum(m_old, jnp.max(s, axis=0, keepdims=True))
        w = jnp.exp2((s - m_new) * SCALE2)
        alpha = jnp.exp2((m_old - m_new) * SCALE2)
        stat[0:1] = m_new
        stat[1:2] = stat[1:2] * alpha + jnp.sum(w, axis=0, keepdims=True)
        acc[...] = acc[...] * alpha + jnp.dot(vt, w.astype(BF), preferred_element_type=F32)

    def rel(table, i):
        r = jnp.int32(table[0])
        for n, v in enumerate(table):
            r = jnp.where(i == n, v, r)
        return r

    def one_query(j, carry):
        row = lax.rem(pos[2] + rel(RING4, j) + NY, NY)
        tq = row * NZ + pos[3]
        first = tq * rows
        n = first + lane
        qs = jnp.zeros((1, rows), jnp.int32)
        qs_first = jnp.int32(0)
        qs_last = jnp.int32(0)
        for p in range(1, P_SIZE):
            qs = jnp.where(n >= starts[p], starts[p], qs)
            qs_first = jnp.where(first >= starts[p], starts[p], qs_first)
            qs_last = jnp.where(first + rows - 1 >= starts[p], starts[p], qs_last)
        stat[0:1] = jnp.full((1, rows), NEG, F32)
        stat[1:2] = jnp.zeros((1, rows), F32)
        acc[...] = jnp.zeros_like(acc)

        def one_key(b, carry2):
            tk = pos[2] * NZ + lax.rem(pos[3] + rel(RING8, b) + NZ, NZ)
            base = tk * rows
            useful = (tk <= tq) & (base + rows - 1 >= qs_first)
            clean = (tk < tq) & (base >= qs_last)

            @pl.when(useful & clean)
            def _():
                fold(qb[j], kb[b], vb[b], None)

            @pl.when(useful & jnp.logical_not(clean))
            def _():
                m = base + lax.broadcasted_iota(jnp.int32, (rows, rows), 0)
                fold(qb[j], kb[b], vb[b], (m >= qs) & (m <= n))

            return carry2

        lax.fori_loop(0, NZ, one_key, 0)

        def one_cache(b, carry2):
            dev = pos[2] * NZ + b
            begin, end, length = jnp.int32(0), jnp.int32(0), jnp.int32(0)
            for p in range(P_SIZE):
                hit = hold[p] == dev
                begin = jnp.where(hit, starts[p], begin)
                end = jnp.where(hit, ends[p], end)
                length = jnp.where(hit, clen[p], length)

            @pl.when((length > 0) & (begin < first + rows) & (end > first))
            def _():
                block = cb.shape[1]
                slot = lax.broadcasted_iota(jnp.int32, (block, rows), 0)
                vt = jnp.transpose(cb[b, :, HD:].astype(F32)).astype(BF)
                fold(qb[j], cb[b, :, :HD], vt, (slot < length) & (n >= begin) & (n < end))

            return carry2

        lax.fori_loop(0, NZ, one_cache, 0)
        m = stat[0:1]
        l = stat[1:2]
        out[j, :HD] = (acc[...] / jnp.where(l > 0.0, l, 1.0)).astype(BF)
        parts = []
        for value in (m, l):
            for _ in range(3):
                piece = value.astype(BF).astype(F32)
                parts.append(piece)
                value = value - piece
        parts.append(jnp.zeros((2, rows), F32))
        out[j, HD:] = jnp.concatenate([jnp.concatenate(parts, axis=0), jnp.zeros((8, rows), F32)], axis=0).astype(BF)
        return carry

    lax.fori_loop(0, NY, one_query, 0)


def attend_call(pos, plen, clen, hold, q, k, v, cache):
    rows, block = 384, cache.shape[1]
    return pl.pallas_call(
        attend_kernel,
        out_shape=jax.ShapeDtypeStruct((NY, HD + 16, rows), BF),
        in_specs=[smem()] * 4 + [hbm()] * 24,
        out_specs=vmem(),
        scratch_shapes=[
            pltpu.VMEM((NY, rows, HD), BF),
            pltpu.VMEM((NZ, rows, HD), BF),
            pltpu.VMEM((NZ, HD, rows), BF),
            pltpu.VMEM((NZ, block, 2 * HD), BF),
            pltpu.VMEM((8, rows), F32),
            pltpu.VMEM((HD, rows), F32),
            pltpu.SemaphoreType.DMA((5,)),
            pltpu.SemaphoreType.DMA((9,)),
            pltpu.SemaphoreType.DMA((9,)),
            pltpu.SemaphoreType.DMA,
        ],
        compiler_params=params(),
        name="attend",
    )(pos, plen, clen, hold, *q, *k, *v, cache)


def combine_kernel(a, b, c, d, out):
    ms, ls = [], []
    for ref in (a, b, c, d):
        tail = ref[HD:].astype(F32)
        ms.append(tail[0:1] + tail[1:2] + tail[2:3])
        ls.append(tail[3:4] + tail[4:5] + tail[5:6])
    top = jnp.maximum(jnp.maximum(ms[0], ms[1]), jnp.maximum(ms[2], ms[3]))
    ws = [l * jnp.exp2((m - top) * SCALE2) for m, l in zip(ms, ls)]
    inv = 1.0 / (ws[0] + ws[1] + ws[2] + ws[3])
    total = None
    for ref, w in zip((a, b, c, d), ws):
        term = ref[:HD].astype(F32) * (w * inv)
        total = term if total is None else total + term
    out[...] = jnp.transpose(total).astype(BF)


def combine_call(pieces):
    rows = pieces[0].shape[1]
    return pl.pallas_call(
        combine_kernel,
        out_shape=jax.ShapeDtypeStruct((rows, HD), BF),
        in_specs=[vmem()] * 4,
        out_specs=vmem(),
        compiler_params=params(),
        name="combine",
    )(*pieces)


def final_kernel(pos, mine, other, hidden, bias, w, out, wbuf, sem):
    copies = [pltpu.make_async_copy(w.at[:, g], wbuf.at[g], sem.at[g]) for g in range(NX * NC)]
    for c in copies:
        c.start()
    for c in copies:
        c.wait()
    total = hidden[...].astype(F32) + bias[...]
    for flip, ref in ((0, mine), (1, other)):
        for k in range(NX):
            g = lax.rem(pos[0] + RING4[k] + NX, NX) * NC + (pos[1] ^ flip)
            wg = wbuf[g].reshape(NY * NZ * 8, HD)
            total += jnp.dot(ref[k], wg, preferred_element_type=F32)
    out[...] = total.astype(BF)


def final_call(pos, mine, other, hidden, bias, w):
    rows = hidden.shape[0]
    return pl.pallas_call(
        final_kernel,
        out_shape=jax.ShapeDtypeStruct((rows, HD), BF),
        in_specs=[smem(), vmem(), vmem(), vmem(), vmem(), hbm()],
        out_specs=vmem(),
        scratch_shapes=[
            pltpu.VMEM((NX * NC, NY * NZ, 8, HD), BF),
            pltpu.SemaphoreType.DMA((NX * NC,)),
        ],
        compiler_params=params(),
        name="final",
    )(pos, mine, other, hidden, bias, w)


def group_gather(block):
    rows, width = block.shape
    a, b, c, d, e = ring4(block, "x")
    mine = jnp.concatenate([a, b, c, d, e], axis=0).reshape(NX, rows, width)
    return mine, lax.ppermute(mine, "c", [(0, 1), (1, 0)])


def token_tables(first, rows, plen, clen):
    n = first + jnp.arange(rows, dtype=jnp.int32)
    ends = jnp.cumsum(plen)
    starts = ends - plen
    prompt = jnp.sum((n[:, None] >= ends[None, :]).astype(jnp.int32), axis=1)
    onehot = prompt[:, None] == jnp.arange(P_SIZE, dtype=jnp.int32)[None, :]
    position = n + jnp.sum(jnp.where(onehot, (clen - starts)[None, :], 0), axis=1)
    half = ROT // 2
    lane = jnp.arange(128, dtype=jnp.int32)
    frequency = 10000.0 ** (-2.0 * (lane % half).astype(F32) / ROT)
    angles = position.astype(F32)[:, None] * frequency[None, :]
    cosine, sine = jnp.cos(angles), jnp.sin(angles)
    cosw = jnp.where(lane < ROT, cosine, 1.0)
    sinl = jnp.where(lane < half, -sine, 0.0)
    sinr = jnp.where((lane >= half) & (lane < ROT), sine, 0.0)
    return cosw, sinl, sinr


def shards(hidden, w_qkv, w_out, qkv_bias, out_bias, gain, lbias, cache_k, cache_v, plen, clen, hold):
    rows = hidden.shape[0]
    x, c, y, z = (lax.axis_index(a) for a in "xcyz")
    pos = jnp.stack([x, c, y, z]).astype(jnp.int32)

    wide = jnp.concatenate(
        [w_qkv.astype(BF).reshape(8, NX * NC, 3 * HD), w_out.astype(BF).reshape(8, NX * NC, HD)], axis=2
    ).transpose(1, 0, 2)
    wide = lax.all_to_all(wide, ("x", "c"), 0, 0, tiled=True)
    w_in, w_o = wide[:, :, : 3 * HD], wide[:, :, 3 * HD :]
    w_z = jnp.concatenate(ring8([w_in], "z")[0], axis=0)
    w_z = w_z.reshape(NZ, 8, 8, 3 * HD)
    w_blocks = ring4(w_z, "y")

    cache = lax.all_gather(jnp.concatenate([cache_k, cache_v], axis=1), "z", axis=0, tiled=False)
    w_o = lax.all_gather(w_o, ("y", "z"), axis=0, tiled=False)

    h_mine, h_other = group_gather(hidden)
    normed = norm_call(pos, h_mine, h_other, gain.reshape(8, 1, HD), lbias.reshape(8, 1, HD))
    tables = token_tables((y * NZ + z) * rows, rows, plen, clen)
    q, k, v = proj_call(pos, normed, qkv_bias.reshape(1, 3 * HD), tables, w_blocks)
    qs = ring4(q, "y")
    ks, vs = ring8([k, v], "z")
    o = attend_call(pos, plen, clen, hold, qs, ks, vs, cache)
    back = [o[0], shift(o[1], "y", -1), shift(o[2], "y", 1), shift(o[3], "y", 2)]
    attended = combine_call(back)
    a_mine, a_other = group_gather(attended)
    return final_call(pos, a_mine, a_other, hidden, out_bias.reshape(1, HD), w_o)


def solution(mesh):
    fine = Mesh(mesh.devices.reshape(NX, NC, NY, NZ), ("x", "c", "y", "z"))
    tok, grp = ("y", "z"), ("x", "c")
    placed = (
        P(tok, grp),
        P(grp + tok, None),
        P(grp + tok, None),
        P(grp),
        P(grp),
        P(),
        P(),
        P(tok, grp),
        P(tok, grp),
        P(),
        P(),
        P(),
    )
    return jax.shard_map(shards, mesh=fine, in_specs=placed, out_specs=P(tok, grp), check_vma=False)
```

```python
import math

import jax
import jax.numpy as jnp
from jax import lax
from jax.experimental import pallas as pl
from jax.experimental.pallas import tpu as pltpu
from jax.sharding import Mesh, PartitionSpec as P

HD = 256
ROT = 64
P_SIZE = 8
NX, NC, NY, NZ = 4, 2, 4, 8
SIZES = {"x": NX, "c": NC, "y": NY, "z": NZ}
NEG = -1e30
SCALE2 = math.log2(math.e) / math.sqrt(HD)
BF = jnp.bfloat16
F32 = jnp.float32


def shift(value, axis, by):
    n = SIZES[axis]
    return lax.ppermute(value, axis, [(i, (i + by) % n) for i in range(n)])


RING4 = (0, -1, 1, 2)
RING8 = (0, -1, 1, -2, 2, -3, 3, 4)


def vmem():
    return pl.BlockSpec(memory_space=pltpu.VMEM)


def smem():
    return pl.BlockSpec(memory_space=pltpu.SMEM)


def hbm():
    return pl.BlockSpec(memory_space=pltpu.HBM)


def params(mb=16):
    return pltpu.CompilerParams(vmem_limit_bytes=mb << 20)


def norm_kernel(whole, gain, bias, out):
    groups, rows, _ = whole.shape
    total = jnp.zeros((rows, 1), F32)
    for g in range(groups):
        total += jnp.sum(whole[g].astype(F32), axis=1, keepdims=True)
    mean = total * (1.0 / (groups * HD))
    square = jnp.zeros((rows, 1), F32)
    for g in range(groups):
        d = whole[g].astype(F32) - mean
        square += jnp.sum(d * d, axis=1, keepdims=True)
    scale = lax.rsqrt(square * (1.0 / (groups * HD)) + 1e-05)
    for g in range(groups):
        d = whole[g].astype(F32) - mean
        out[g] = (d * scale * gain[g] + bias[g]).astype(BF)


def norm_call(whole, gain, bias):
    return pl.pallas_call(
        norm_kernel,
        out_shape=jax.ShapeDtypeStruct(whole.shape, BF),
        in_specs=[vmem()] * 3,
        out_specs=vmem(),
        compiler_params=params(),
        name="norm",
    )(whole, gain, bias)


def prep_kernel(a, b, out):
    for g in range(NX * NC):
        out[g, :, : 3 * HD] = a[:, g * 3 * HD : (g + 1) * 3 * HD].astype(BF)
        out[g, :, 3 * HD :] = b[:, g * HD : (g + 1) * HD].astype(BF)


def prep_call(a, b):
    return pl.pallas_call(
        prep_kernel,
        out_shape=jax.ShapeDtypeStruct((NX * NC, 8, 4 * HD), BF),
        in_specs=[vmem(), vmem()],
        out_specs=vmem(),
        compiler_params=params(8),
        name="prep",
    )(a, b)


def proj_kernel(pos, normed, bias, cosw, sinl, sinr, *refs):
    blocks, (q_out, kv_out, wbuf, sem) = refs[:8], refs[8:]
    copies = []
    for n, ref in enumerate(blocks):
        row = lax.rem(pos[2] + RING4[n // 2] + NY, NY) * NZ
        for i in range(NZ // 2):
            at = row + lax.rem(pos[3] + RING8[(n % 2) * (NZ // 2) + i] + NZ, NZ)
            copies.append(pltpu.make_async_copy(ref.at[i], wbuf.at[:, at], sem.at[len(copies)]))
    for c in copies:
        c.start()
    for c in copies:
        c.wait()
    rows = normed.shape[1]

    def part(n):
        total = jnp.broadcast_to(bias[:, n * HD : (n + 1) * HD], (rows, HD))
        for g in range(NX * NC):
            w = wbuf[g, :, :, n * HD : (n + 1) * HD].reshape(NY * NZ * 8, HD)
            total += jnp.dot(normed[g], w, preferred_element_type=F32)
        return total

    def rotated(value):
        head = value[:, :128]
        back = pltpu.roll(head, 128 - ROT // 2, 1)
        fwd = pltpu.roll(head, ROT // 2, 1)
        return head * cosw[...] + back * sinl[...] + fwd * sinr[...]

    q = part(0)
    head, tail = rotated(q).astype(BF), q[:, 128:].astype(BF)
    for i in range(NY):
        q_out[i, :, :128] = head
        q_out[i, :, 128:] = tail
    k = part(1)
    kv_out[:rows, :128] = rotated(k).astype(BF)
    kv_out[:rows, 128:] = k[:, 128:].astype(BF)
    kv_out[rows:] = part(2).astype(BF)


def proj_call(pos, normed, bias, tables, blocks):
    rows = normed.shape[1]
    return pl.pallas_call(
        proj_kernel,
        out_shape=(
            jax.ShapeDtypeStruct((NY, rows, HD), BF),
            jax.ShapeDtypeStruct((2 * rows, HD), BF),
        ),
        in_specs=[smem()] + [vmem()] * 5 + [hbm()] * 8,
        out_specs=(vmem(), vmem()),
        scratch_shapes=[
            pltpu.VMEM((NX * NC, NY * NZ, 8, 3 * HD), BF),
            pltpu.SemaphoreType.DMA((NY * NZ,)),
        ],
        compiler_params=params(24),
        name="proj",
    )(pos, normed, bias, *tables, *blocks)


def attend_call(pos, plen, clen, hold, q, blocks, shifts, cache=None, state=None, last=False):
    rows = q.shape[1]
    flat, where = [], []
    for b in blocks:
        if isinstance(b, tuple):
            where.append((len(flat), 0, len(flat) + 1, 0))
            flat += list(b)
        else:
            where.append((len(flat), 0, len(flat), rows))
            flat.append(b)

    def kernel(pos, plen, clen, hold, q, *refs):
        refs = list(refs)
        kv = [refs.pop(0) for _ in flat]
        cb = refs.pop(0) if cache is not None else None
        old = (refs.pop(0), refs.pop(0)) if state is not None else None
        cbuf, csem = (refs.pop(), refs.pop())[::-1] if cache is not None else (None, None)
        if last:
            out, acc, stat, vt = refs
        else:
            acc, stat, vt = refs
        starts, ends = [], []
        run = jnp.int32(0)
        for p in range(P_SIZE):
            starts.append(run)
            run = run + plen[p]
            ends.append(run)
        if old is None:
            acc[...] = jnp.zeros_like(acc)
            stat[:, 0:1] = jnp.full((NY, 1, rows), NEG, F32)
            stat[:, 1:2] = jnp.zeros((NY, 1, rows), F32)
        else:
            acc[...] = old[0][...]
            stat[...] = old[1][...]
        lane = lax.broadcasted_iota(jnp.int32, (1, rows), 1)

        def limits(j):
            first = (j * NZ + pos[3]) * rows
            n = first + lane
            qs = jnp.zeros((1, rows), jnp.int32)
            qs_first = jnp.int32(0)
            for p in range(1, P_SIZE):
                qs = jnp.where(n >= starts[p], starts[p], qs)
                qs_first = jnp.where(first >= starts[p], starts[p], qs_first)
            return first, n, qs, qs_first

        def fold(j, k, count, low, high):
            index = lax.broadcasted_iota(jnp.int32, (count, rows), 0)
            for cut in (slice(0, rows),):
                s = lax.dot_general(k, q[j, cut], (((1,), (1,)), ((), ())), preferred_element_type=F32)
                s = jnp.where((index >= low[:, cut]) & (index <= high[:, cut]), s, NEG)
                m_old = stat[j, 0:1, cut]
                m_new = jnp.maximum(m_old, jnp.max(s, axis=0, keepdims=True))
                w = jnp.exp2((s - m_new) * SCALE2)
                alpha = jnp.exp2((m_old - m_new) * SCALE2)
                stat[j, 0:1, cut] = m_new
                stat[j, 1:2, cut] = stat[j, 1:2, cut] * alpha + jnp.sum(w, axis=0, keepdims=True)
                acc[j, :, cut] = acc[j, :, cut] * alpha + jnp.dot(
                    vt[:, :count], w.astype(BF), preferred_element_type=F32
                )

        for (ki, ko, vi, vo), by in zip(where, shifts):
            tk = pos[2] * NZ + lax.rem(pos[3] + by + NZ, NZ)
            base = tk * rows
            vt[...] = jnp.transpose(kv[vi][vo : vo + rows].astype(F32)).astype(BF)

            def one_query(j, carry):
                first, n, qs, qs_first = limits(j)

                @pl.when((base <= first) & (base + rows - 1 >= qs_first))
                def _():
                    fold(j, kv[ki][ko : ko + rows], rows, qs - base, n - base)

                return carry

            lax.fori_loop(pos[2], NY, one_query, 0)

        if cb is not None:
            count = cbuf.shape[0] // 2

            def one_cache(b, carry):
                dev = pos[2] * NZ + b
                begin, end, length = jnp.int32(0), jnp.int32(0), jnp.int32(0)
                for p in range(P_SIZE):
                    hit = hold[p] == dev
                    begin = jnp.where(hit, starts[p], begin)
                    end = jnp.where(hit, ends[p], end)
                    length = jnp.where(hit, clen[p], length)

                @pl.when(length > 0)
                def _():
                    copy = pltpu.make_async_copy(cb.at[b, pl.ds(0, 2 * count)], cbuf, csem)
                    copy.start()
                    copy.wait()
                    vt[:, :count] = jnp.transpose(cbuf[count:].astype(F32)).astype(BF)

                    def one_query(j, carry2):
                        first, n, qs, qs_first = limits(j)

                        @pl.when((begin < first + rows) & (end > first))
                        def _():
                            ours = (n >= begin) & (n < end)
                            high = jnp.where(ours, length - 1, -1)
                            fold(j, cbuf[:count], count, jnp.zeros_like(high), high)

                        return carry2

                    lax.fori_loop(0, NY, one_query, 0)

                return carry

            lax.fori_loop(0, NZ, one_cache, 0)

        if last:

            def finish(j, carry):
                m = stat[j, 0:1]
                l = stat[j, 1:2]
                out[j, :HD] = (acc[j] * (1.0 / jnp.where(l > 0.0, l, 1.0))).astype(BF)
                parts = []
                for value in (m, l):
                    for _ in range(3):
                        piece = value.astype(BF).astype(F32)
                        parts.append(piece)
                        value = value - piece
                parts.append(jnp.zeros((10, rows), F32))
                out[j, HD:] = jnp.concatenate(parts, axis=0).astype(BF)
                return carry

            lax.fori_loop(0, NY, finish, 0)

    acc_type = jax.ShapeDtypeStruct((NY, HD, rows), F32)
    stat_type = jax.ShapeDtypeStruct((NY, 8, rows), F32)
    scratch = [pltpu.VMEM((HD, rows), BF)]
    if last:
        out_shape = jax.ShapeDtypeStruct((NY, HD + 16, rows), BF)
        scratch = [pltpu.VMEM(t.shape, F32) for t in (acc_type, stat_type)] + scratch
    else:
        out_shape = (acc_type, stat_type)
    if cache is not None:
        scratch += [pltpu.VMEM((512, HD), BF), pltpu.SemaphoreType.DMA]
    specs = [vmem()] * (1 + len(flat)) + ([hbm()] if cache is not None else []) + [vmem()] * (2 if state is not None else 0)
    ins = [q] + flat + ([cache] if cache is not None else []) + (list(state) if state is not None else [])
    alias = {} if last or state is None else {4 + len(ins) - 2: 0, 4 + len(ins) - 1: 1}
    work = len(blocks) * 2.5 * rows * rows * HD * 4
    return pl.pallas_call(
        kernel,
        out_shape=out_shape,
        in_specs=[smem()] * 4 + specs,
        out_specs=vmem() if last else (vmem(), vmem()),
        scratch_shapes=scratch,
        input_output_aliases=alias,
        compiler_params=params(24),
        name="attend",
    )(pos, plen, clen, hold, *ins)


def combine_kernel(a, b, c, d, out):
    ms, ls = [], []
    for ref in (a, b, c, d):
        tail = ref[HD:].astype(F32)
        ms.append(tail[0:1] + tail[1:2] + tail[2:3])
        ls.append(tail[3:4] + tail[4:5] + tail[5:6])
    top = jnp.maximum(jnp.maximum(ms[0], ms[1]), jnp.maximum(ms[2], ms[3]))
    ws = [l * jnp.exp2((m - top) * SCALE2) for m, l in zip(ms, ls)]
    inv = 1.0 / (ws[0] + ws[1] + ws[2] + ws[3])
    total = None
    for ref, w in zip((a, b, c, d), ws):
        term = ref[:HD].astype(F32) * (w * inv)
        total = term if total is None else total + term
    done = jnp.transpose(total).astype(BF)
    for i in range(NX):
        out[i] = done


def combine_call(pieces):
    rows = pieces[0].shape[1]
    return pl.pallas_call(
        combine_kernel,
        out_shape=jax.ShapeDtypeStruct((NX, rows, HD), BF),
        in_specs=[vmem()] * 4,
        out_specs=vmem(),
        compiler_params=params(),
        name="combine",
    )(*pieces)


def final_kernel(pos, mine, other, hidden, bias, w, out):
    total = hidden[...].astype(F32) + bias[...]
    for flip, ref in ((0, mine), (1, other)):
        for k in range(NX):
            g = k * NC + (pos[1] ^ flip)
            wg = w[:, :, g].reshape(NY * NZ * 8, HD)
            total += jnp.dot(ref[k], wg, preferred_element_type=F32)
    out[...] = total.astype(BF)


def final_call(pos, mine, other, hidden, bias, w):
    rows = hidden.shape[0]
    return pl.pallas_call(
        final_kernel,
        out_shape=jax.ShapeDtypeStruct((rows, HD), BF),
        in_specs=[smem()] + [vmem()] * 5,
        out_specs=vmem(),
        compiler_params=params(),
        name="final",
    )(pos, mine, other, hidden, bias, w)


def spread(block, axis):
    n = SIZES[axis]
    return lax.all_to_all(jnp.broadcast_to(block[None], (n,) + block.shape), axis, 0, 0, tiled=True)


def z_gather(block):
    half = block.shape[0] // 2
    parts = [block]
    right, left = block, block
    for _ in range(3):
        right, left = shift(right, "z", 1), shift(left, "z", -1)
        parts += [right, left]
    parts += [shift(right[:half], "z", 1), shift(left[half:], "z", -1)]
    shape = (NZ // 2,) + block.shape
    return jnp.concatenate(parts[:4], axis=0).reshape(shape), jnp.concatenate(parts[4:], axis=0).reshape(shape)


def token_tables(first, rows, plen, clen):
    n = first + jnp.arange(rows, dtype=jnp.int32)
    ends = jnp.cumsum(plen)
    starts = ends - plen
    prompt = jnp.sum((n[:, None] >= ends[None, :]).astype(jnp.int32), axis=1)
    onehot = prompt[:, None] == jnp.arange(P_SIZE, dtype=jnp.int32)[None, :]
    position = n + jnp.sum(jnp.where(onehot, (clen - starts)[None, :], 0), axis=1)
    half = ROT // 2
    lane = jnp.arange(128, dtype=jnp.int32)
    frequency = 10000.0 ** (-2.0 * (lane % half).astype(F32) / ROT)
    angles = position.astype(F32)[:, None] * frequency[None, :]
    cosine, sine = jnp.cos(angles), jnp.sin(angles)
    cosw = jnp.where(lane < ROT, cosine, 1.0)
    sinl = jnp.where(lane < half, -sine, 0.0)
    sinr = jnp.where((lane >= half) & (lane < ROT), sine, 0.0)
    return cosw, sinl, sinr


def shards(hidden, w_qkv, w_out, qkv_bias, out_bias, gain, lbias, cache_k, cache_v, plen, clen, hold):
    rows = hidden.shape[0]
    x, c, y, z = (lax.axis_index(a) for a in "xcyz")
    pos = jnp.stack([x, c, y, z]).astype(jnp.int32)

    wide = lax.all_to_all(prep_call(w_qkv, w_out), ("x", "c"), 0, 0, tiled=True)
    w_in, w_o = wide[:, :, : 3 * HD], wide[:, :, 3 * HD :].reshape(8 * NX * NC, HD)
    near, far = z_gather(w_in)
    near, far, w_o, cache_k, cache_v = lax.optimization_barrier((near, far, w_o, cache_k, cache_v))
    ups, downs = [shift(near, "y", 1)], [shift(near, "y", -1)]
    ups, downs = ups + [shift(far, "y", 1)], downs + [shift(far, "y", -1)]
    slots = cache_k.shape[0]
    table = lax.all_gather(jnp.concatenate([cache_k, cache_v, w_o], axis=0), "z", axis=0, tiled=False)
    whole = lax.all_gather(hidden, ("x", "c"), axis=0, tiled=False)
    normed = norm_call(whole, gain.reshape(8, 1, HD), lbias.reshape(8, 1, HD))
    tables = token_tables((y * NZ + z) * rows, rows, plen, clen)
    w_blocks = [near, far, ups[0], ups[1], downs[0], downs[1], shift(ups[0], "y", 1), shift(downs[1], "y", -1)]

    q4, kv = proj_call(pos, normed, qkv_bias.reshape(1, 3 * HD), tables, w_blocks)
    q = lax.all_to_all(q4, "y", 0, 0, tiled=True)
    q, table = lax.optimization_barrier((q, table))
    w_o = table[:, 2 * slots :].reshape(NZ, NX * NC, 8, HD)
    w_o = lax.all_gather(w_o, "y", axis=0, tiled=False)
    meta = (pos, plen, clen, hold, q)
    r1, l1 = shift(kv, "z", 1), shift(kv, "z", -1)
    r2, l2 = shift(r1, "z", 1), shift(l1, "z", -1)
    state = attend_call(*meta, [kv, r1, l1], (0, -1, 1))
    r2, l2, state = lax.optimization_barrier((r2, l2, state))
    r3, l3 = shift(r2, "z", 1), shift(l2, "z", -1)
    state = attend_call(*meta, [r2, l2], (-2, 2), state=state)
    r3, l3, state = lax.optimization_barrier((r3, l3, state))
    far = shift(r3, "z", 1)
    state = attend_call(*meta, [r3, l3], (-3, 3), cache=table, state=state)
    far, state, w_o = lax.optimization_barrier((far, state, w_o))
    o = attend_call(*meta, [far], (4,), state=state, last=True)
    rows_of = [lax.dynamic_index_in_dim(o, lax.rem(y + by + NY, NY), 0, keepdims=False) for by in RING4]
    back = [rows_of[0], shift(rows_of[1], "y", -1), shift(rows_of[2], "y", 1), shift(rows_of[3], "y", 2)]
    a_mine = lax.all_to_all(combine_call(back), "x", 0, 0, tiled=True)
    a_other = lax.ppermute(a_mine, "c", [(0, 1), (1, 0)])
    return final_call(pos, a_mine, a_other, hidden, out_bias.reshape(1, HD), w_o)


def solution(mesh):
    fine = Mesh(mesh.devices.reshape(NX, NC, NY, NZ), ("x", "c", "y", "z"))
    tok, grp = ("y", "z"), ("x", "c")
    placed = (
        P(tok, grp),
        P(grp + tok, None),
        P(grp + tok, None),
        P(grp),
        P(grp),
        P(),
        P(),
        P(tok, grp),
        P(tok, grp),
        P(),
        P(),
        P(),
    )
    return jax.shard_map(shards, mesh=fine, in_specs=placed, out_specs=P(tok, grp), check_vma=False)
```

```python
import math

import jax
import jax.numpy as jnp
from jax import lax
from jax.experimental import pallas as pl
from jax.experimental.pallas import tpu as pltpu
from jax.sharding import Mesh, PartitionSpec as P

HD = 256
ROT = 64
P_SIZE = 8
NX, NC, NY, NZ = 4, 2, 4, 8
SIZES = {"x": NX, "c": NC, "y": NY, "z": NZ}
NEG = -1e30
SCALE2 = math.log2(math.e) / math.sqrt(HD)
BF = jnp.bfloat16
F32 = jnp.float32


def shift(value, axis, by):
    n = SIZES[axis]
    return lax.ppermute(value, axis, [(i, (i + by) % n) for i in range(n)])


RING4 = (0, -1, 1, 2)
RING8 = (0, -1, 1, -2, 2, -3, 3, 4)


def vmem():
    return pl.BlockSpec(memory_space=pltpu.VMEM)


def smem():
    return pl.BlockSpec(memory_space=pltpu.SMEM)


def hbm():
    return pl.BlockSpec(memory_space=pltpu.HBM)


def params(mb=16):
    return pltpu.CompilerParams(vmem_limit_bytes=mb << 20)


def norm_kernel(whole, gain, bias, out):
    groups, rows, _ = whole.shape
    total = jnp.zeros((rows, 1), F32)
    for g in range(groups):
        total += jnp.sum(whole[g].astype(F32), axis=1, keepdims=True)
    mean = total * (1.0 / (groups * HD))
    square = jnp.zeros((rows, 1), F32)
    for g in range(groups):
        d = whole[g].astype(F32) - mean
        square += jnp.sum(d * d, axis=1, keepdims=True)
    scale = lax.rsqrt(square * (1.0 / (groups * HD)) + 1e-05)
    for g in range(groups):
        d = whole[g].astype(F32) - mean
        out[g] = (d * scale * gain[g] + bias[g]).astype(BF)


def norm_call(whole, gain, bias):
    return pl.pallas_call(
        norm_kernel,
        out_shape=jax.ShapeDtypeStruct(whole.shape, BF),
        in_specs=[vmem()] * 3,
        out_specs=vmem(),
        compiler_params=params(),
        name="norm",
    )(whole, gain, bias)


def prep_kernel(a, b, out):
    for g in range(NX * NC):
        out[g, :, : 3 * HD] = a[:, g * 3 * HD : (g + 1) * 3 * HD].astype(BF)
        out[g, :, 3 * HD :] = b[:, g * HD : (g + 1) * HD].astype(BF)


def prep_call(a, b):
    return pl.pallas_call(
        prep_kernel,
        out_shape=jax.ShapeDtypeStruct((NX * NC, 8, 4 * HD), BF),
        in_specs=[vmem(), vmem()],
        out_specs=vmem(),
        compiler_params=params(8),
        name="prep",
    )(a, b)


def proj_kernel(pos, normed, bias, cosw, sinl, sinr, *refs):
    blocks, (q_out, kv_out, wbuf, sem) = refs[:8], refs[8:]
    copies = []
    for n, ref in enumerate(blocks):
        row = lax.rem(pos[2] + RING4[n // 2] + NY, NY) * NZ
        for i in range(NZ // 2):
            at = row + lax.rem(pos[3] + RING8[(n % 2) * (NZ // 2) + i] + NZ, NZ)
            copies.append(pltpu.make_async_copy(ref.at[i], wbuf.at[:, at], sem.at[len(copies)]))
    for c in copies:
        c.start()
    for c in copies:
        c.wait()
    rows = normed.shape[1]

    def part(n):
        total = jnp.broadcast_to(bias[:, n * HD : (n + 1) * HD], (rows, HD))
        for g in range(NX * NC):
            w = wbuf[g, :, :, n * HD : (n + 1) * HD].reshape(NY * NZ * 8, HD)
            total += jnp.dot(normed[g], w, preferred_element_type=F32)
        return total

    def rotated(value):
        head = value[:, :128]
        back = pltpu.roll(head, 128 - ROT // 2, 1)
        fwd = pltpu.roll(head, ROT // 2, 1)
        return head * cosw[...] + back * sinl[...] + fwd * sinr[...]

    q = part(0)
    head, tail = rotated(q).astype(BF), q[:, 128:].astype(BF)
    for i in range(NY):
        q_out[i, :, :128] = head
        q_out[i, :, 128:] = tail
    k = part(1)
    kv_out[:rows, :128] = rotated(k).astype(BF)
    kv_out[:rows, 128:] = k[:, 128:].astype(BF)
    kv_out[rows:] = part(2).astype(BF)


def proj_call(pos, normed, bias, tables, blocks):
    rows = normed.shape[1]
    return pl.pallas_call(
        proj_kernel,
        out_shape=(
            jax.ShapeDtypeStruct((NY, rows, HD), BF),
            jax.ShapeDtypeStruct((2 * rows, HD), BF),
        ),
        in_specs=[smem()] + [vmem()] * 5 + [hbm()] * 8,
        out_specs=(vmem(), vmem()),
        scratch_shapes=[
            pltpu.VMEM((NX * NC, NY * NZ, 8, 3 * HD), BF),
            pltpu.SemaphoreType.DMA((NY * NZ,)),
        ],
        compiler_params=params(24),
        name="proj",
    )(pos, normed, bias, *tables, *blocks)


def attend_call(pos, plen, clen, hold, q, blocks, shifts, cache=None, state=None, last=False):
    rows = q.shape[1]
    flat, where = [], []
    for b in blocks:
        if isinstance(b, tuple):
            where.append((len(flat), 0, len(flat) + 1, 0))
            flat += list(b)
        else:
            where.append((len(flat), 0, len(flat), rows))
            flat.append(b)

    def kernel(pos, plen, clen, hold, q, *refs):
        refs = list(refs)
        kv = [refs.pop(0) for _ in flat]
        cb = refs.pop(0) if cache is not None else None
        old = (refs.pop(0), refs.pop(0)) if state is not None else None
        cbuf, csem = (refs.pop(), refs.pop())[::-1] if cache is not None else (None, None)
        if last:
            out, acc, stat, vt = refs
        else:
            acc, stat, vt = refs
        starts, ends = [], []
        run = jnp.int32(0)
        for p in range(P_SIZE):
            starts.append(run)
            run = run + plen[p]
            ends.append(run)
        if old is None:
            acc[...] = jnp.zeros_like(acc)
            stat[:, 0:1] = jnp.full((NY, 1, rows), NEG, F32)
            stat[:, 1:2] = jnp.zeros((NY, 1, rows), F32)
        else:
            acc[...] = old[0][...]
            stat[...] = old[1][...]
        lane = lax.broadcasted_iota(jnp.int32, (1, rows), 1)

        def limits(j):
            first = (j * NZ + pos[3]) * rows
            n = first + lane
            qs = jnp.zeros((1, rows), jnp.int32)
            qs_first = jnp.int32(0)
            for p in range(1, P_SIZE):
                qs = jnp.where(n >= starts[p], starts[p], qs)
                qs_first = jnp.where(first >= starts[p], starts[p], qs_first)
            return first, n, qs, qs_first

        def fold(j, k, count, low, high):
            index = lax.broadcasted_iota(jnp.int32, (count, rows), 0)
            for cut in (slice(0, rows),):
                s = lax.dot_general(k, q[j, cut], (((1,), (1,)), ((), ())), preferred_element_type=F32)
                s = jnp.where((index >= low[:, cut]) & (index <= high[:, cut]), s, NEG)
                m_old = stat[j, 0:1, cut]
                m_new = jnp.maximum(m_old, jnp.max(s, axis=0, keepdims=True))
                w = jnp.exp2((s - m_new) * SCALE2)
                alpha = jnp.exp2((m_old - m_new) * SCALE2)
                stat[j, 0:1, cut] = m_new
                stat[j, 1:2, cut] = stat[j, 1:2, cut] * alpha + jnp.sum(w, axis=0, keepdims=True)
                acc[j, :, cut] = acc[j, :, cut] * alpha + jnp.dot(
                    vt[:, :count], w.astype(BF), preferred_element_type=F32
                )

        for (ki, ko, vi, vo), by in zip(where, shifts):
            tk = pos[2] * NZ + lax.rem(pos[3] + by + NZ, NZ)
            base = tk * rows
            vt[...] = jnp.transpose(kv[vi][vo : vo + rows].astype(F32)).astype(BF)

            def one_query(j, carry):
                first, n, qs, qs_first = limits(j)

                @pl.when((base <= first) & (base + rows - 1 >= qs_first))
                def _():
                    fold(j, kv[ki][ko : ko + rows], rows, qs - base, n - base)

                return carry

            lax.fori_loop(pos[2], NY, one_query, 0)

        if cb is not None:
            count = cbuf.shape[0] // 2

            def one_cache(b, carry):
                dev = pos[2] * NZ + b
                begin, end, length = jnp.int32(0), jnp.int32(0), jnp.int32(0)
                for p in range(P_SIZE):
                    hit = hold[p] == dev
                    begin = jnp.where(hit, starts[p], begin)
                    end = jnp.where(hit, ends[p], end)
                    length = jnp.where(hit, clen[p], length)

                @pl.when(length > 0)
                def _():
                    copy = pltpu.make_async_copy(cb.at[b, pl.ds(0, 2 * count)], cbuf, csem)
                    copy.start()
                    copy.wait()
                    vt[:, :count] = jnp.transpose(cbuf[count:].astype(F32)).astype(BF)

                    def one_query(j, carry2):
                        first, n, qs, qs_first = limits(j)

                        @pl.when((begin < first + rows) & (end > first))
                        def _():
                            ours = (n >= begin) & (n < end)
                            high = jnp.where(ours, length - 1, -1)
                            fold(j, cbuf[:count], count, jnp.zeros_like(high), high)

                        return carry2

                    lax.fori_loop(0, NY, one_query, 0)

                return carry

            lax.fori_loop(0, NZ, one_cache, 0)

        if last:

            def finish(j, carry):
                m = stat[j, 0:1]
                l = stat[j, 1:2]
                out[j, :HD] = (acc[j] * (1.0 / jnp.where(l > 0.0, l, 1.0))).astype(BF)
                parts = []
                for value in (m, l):
                    for _ in range(3):
                        piece = value.astype(BF).astype(F32)
                        parts.append(piece)
                        value = value - piece
                parts.append(jnp.zeros((10, rows), F32))
                out[j, HD:] = jnp.concatenate(parts, axis=0).astype(BF)
                return carry

            lax.fori_loop(0, NY, finish, 0)

    acc_type = jax.ShapeDtypeStruct((NY, HD, rows), F32)
    stat_type = jax.ShapeDtypeStruct((NY, 8, rows), F32)
    scratch = [pltpu.VMEM((HD, rows), BF)]
    if last:
        out_shape = jax.ShapeDtypeStruct((NY, HD + 16, rows), BF)
        scratch = [pltpu.VMEM(t.shape, F32) for t in (acc_type, stat_type)] + scratch
    else:
        out_shape = (acc_type, stat_type)
    if cache is not None:
        scratch += [pltpu.VMEM((512, HD), BF), pltpu.SemaphoreType.DMA]
    specs = [vmem()] * (1 + len(flat)) + ([hbm()] if cache is not None else []) + [vmem()] * (2 if state is not None else 0)
    ins = [q] + flat + ([cache] if cache is not None else []) + (list(state) if state is not None else [])
    alias = {} if last or state is None else {4 + len(ins) - 2: 0, 4 + len(ins) - 1: 1}
    work = len(blocks) * 2.5 * rows * rows * HD * 4
    return pl.pallas_call(
        kernel,
        out_shape=out_shape,
        in_specs=[smem()] * 4 + specs,
        out_specs=vmem() if last else (vmem(), vmem()),
        scratch_shapes=scratch,
        input_output_aliases=alias,
        compiler_params=params(24),
        name="attend",
    )(pos, plen, clen, hold, *ins)


def combine_kernel(a, b, c, d, out):
    ms, ls = [], []
    for ref in (a, b, c, d):
        tail = ref[HD:].astype(F32)
        ms.append(tail[0:1] + tail[1:2] + tail[2:3])
        ls.append(tail[3:4] + tail[4:5] + tail[5:6])
    top = jnp.maximum(jnp.maximum(ms[0], ms[1]), jnp.maximum(ms[2], ms[3]))
    ws = [l * jnp.exp2((m - top) * SCALE2) for m, l in zip(ms, ls)]
    inv = 1.0 / (ws[0] + ws[1] + ws[2] + ws[3])
    total = None
    for ref, w in zip((a, b, c, d), ws):
        term = ref[:HD].astype(F32) * (w * inv)
        total = term if total is None else total + term
    done = jnp.transpose(total).astype(BF)
    for i in range(NX):
        out[i] = done


def combine_call(pieces):
    rows = pieces[0].shape[1]
    return pl.pallas_call(
        combine_kernel,
        out_shape=jax.ShapeDtypeStruct((NX, rows, HD), BF),
        in_specs=[vmem()] * 4,
        out_specs=vmem(),
        compiler_params=params(),
        name="combine",
    )(*pieces)


def final_kernel(pos, mine, other, hidden, bias, w, out):
    total = hidden[...].astype(F32) + bias[...]
    for flip, ref in ((0, mine), (1, other)):
        for k in range(NX):
            g = k * NC + (pos[1] ^ flip)
            wg = w[:, :, g].reshape(NY * NZ * 8, HD)
            total += jnp.dot(ref[k], wg, preferred_element_type=F32)
    out[...] = total.astype(BF)


def final_call(pos, mine, other, hidden, bias, w):
    rows = hidden.shape[0]
    return pl.pallas_call(
        final_kernel,
        out_shape=jax.ShapeDtypeStruct((rows, HD), BF),
        in_specs=[smem()] + [vmem()] * 5,
        out_specs=vmem(),
        compiler_params=params(),
        name="final",
    )(pos, mine, other, hidden, bias, w)


def spread(block, axis):
    n = SIZES[axis]
    return lax.all_to_all(jnp.broadcast_to(block[None], (n,) + block.shape), axis, 0, 0, tiled=True)


def z_gather(block):
    half = block.shape[0] // 2
    parts = [block]
    right, left = block, block
    for _ in range(3):
        right, left = shift(right, "z", 1), shift(left, "z", -1)
        parts += [right, left]
    parts += [shift(right[:half], "z", 1), shift(left[half:], "z", -1)]
    shape = (NZ // 2,) + block.shape
    return jnp.concatenate(parts[:4], axis=0).reshape(shape), jnp.concatenate(parts[4:], axis=0).reshape(shape)


def token_tables(first, rows, plen, clen):
    n = first + jnp.arange(rows, dtype=jnp.int32)
    ends = jnp.cumsum(plen)
    starts = ends - plen
    prompt = jnp.sum((n[:, None] >= ends[None, :]).astype(jnp.int32), axis=1)
    onehot = prompt[:, None] == jnp.arange(P_SIZE, dtype=jnp.int32)[None, :]
    position = n + jnp.sum(jnp.where(onehot, (clen - starts)[None, :], 0), axis=1)
    half = ROT // 2
    lane = jnp.arange(128, dtype=jnp.int32)
    frequency = 10000.0 ** (-2.0 * (lane % half).astype(F32) / ROT)
    angles = position.astype(F32)[:, None] * frequency[None, :]
    cosine, sine = jnp.cos(angles), jnp.sin(angles)
    cosw = jnp.where(lane < ROT, cosine, 1.0)
    sinl = jnp.where(lane < half, -sine, 0.0)
    sinr = jnp.where((lane >= half) & (lane < ROT), sine, 0.0)
    return cosw, sinl, sinr


def shards(hidden, w_qkv, w_out, qkv_bias, out_bias, gain, lbias, cache_k, cache_v, plen, clen, hold):
    rows = hidden.shape[0]
    x, c, y, z = (lax.axis_index(a) for a in "xcyz")
    pos = jnp.stack([x, c, y, z]).astype(jnp.int32)

    wide = lax.all_to_all(prep_call(w_qkv, w_out), ("x", "c"), 0, 0, tiled=True)
    w_in, w_o = wide[:, :, : 3 * HD], wide[:, :, 3 * HD :].reshape(8 * NX * NC, HD)
    near, far = z_gather(w_in)
    near, far, w_o, cache_k, cache_v = lax.optimization_barrier((near, far, w_o, cache_k, cache_v))
    ups, downs = [shift(near, "y", 1)], [shift(near, "y", -1)]
    ups, downs = ups + [shift(far, "y", 1)], downs + [shift(far, "y", -1)]
    slots = cache_k.shape[0]
    table = lax.all_gather(jnp.concatenate([cache_k, cache_v, w_o], axis=0), "z", axis=0, tiled=False)
    whole = lax.all_gather(hidden, ("x", "c"), axis=0, tiled=False)
    normed = norm_call(whole, gain.reshape(8, 1, HD), lbias.reshape(8, 1, HD))
    tables = token_tables((y * NZ + z) * rows, rows, plen, clen)
    w_blocks = [near, far, ups[0], ups[1], downs[0], downs[1], shift(ups[0], "y", 1), shift(downs[1], "y", -1)]

    q4, kv = proj_call(pos, normed, qkv_bias.reshape(1, 3 * HD), tables, w_blocks)
    q = lax.all_to_all(q4, "y", 0, 0, tiled=True)
    meta = (pos, plen, clen, hold, q)
    r1, l1 = shift(kv, "z", 1), shift(kv, "z", -1)
    r2, l2 = shift(r1, "z", 1), shift(l1, "z", -1)
    state = attend_call(*meta, [kv, r1, l1], (0, -1, 1))
    r2, l2, state, table = lax.optimization_barrier((r2, l2, state, table))
    w_o = table[:, 2 * slots :].reshape(NZ, NX * NC, 8, HD)
    w_o = lax.all_gather(w_o, "y", axis=0, tiled=False)
    r3, l3 = shift(r2, "z", 1), shift(l2, "z", -1)
    state = attend_call(*meta, [r2, l2], (-2, 2), state=state)
    r3, l3, state = lax.optimization_barrier((r3, l3, state))
    far = shift(r3, "z", 1)
    state = attend_call(*meta, [r3, l3], (-3, 3), cache=table, state=state)
    far, state, w_o = lax.optimization_barrier((far, state, w_o))
    o = attend_call(*meta, [far], (4,), state=state, last=True)
    rows_of = [lax.dynamic_index_in_dim(o, lax.rem(y + by + NY, NY), 0, keepdims=False) for by in RING4]
    back = [rows_of[0], shift(rows_of[1], "y", -1), shift(rows_of[2], "y", 1), shift(rows_of[3], "y", 2)]
    a_mine = lax.all_to_all(combine_call(back), "x", 0, 0, tiled=True)
    a_other = lax.ppermute(a_mine, "c", [(0, 1), (1, 0)])
    return final_call(pos, a_mine, a_other, hidden, out_bias.reshape(1, HD), w_o)


def solution(mesh):
    fine = Mesh(mesh.devices.reshape(NX, NC, NY, NZ), ("x", "c", "y", "z"))
    tok, grp = ("y", "z"), ("x", "c")
    placed = (
        P(tok, grp),
        P(grp + tok, None),
        P(grp + tok, None),
        P(grp),
        P(grp),
        P(),
        P(),
        P(tok, grp),
        P(tok, grp),
        P(),
        P(),
        P(),
    )
    return jax.shard_map(shards, mesh=fine, in_specs=placed, out_specs=P(tok, grp), check_vma=False)
```
